256 devices in a mesh: pair: 64 (over y, z, x_hi), day: 4 (over x_lo, core).
Axes of the slice: x: 4 (x_hi: 2, x_lo: 2; x = x_hi * 2 + x_lo), y: 4, z: 8, core: 2. Of those that a mesh axis runs over, the one named last changes fastest.
Arguments:
- spectra: bfloat16 [8, 64, 128, 8192], P('day', 'pair'), may hold values from -6 to 6
- pair_mask: int32 [64, 2], P('pair'), may hold values 0 or 1
- window_of_day: int32 [8], replicated, may hold values from 0 to 1, as said below
- band_weight: float32 [8], replicated, may hold values from 0.5 to 4
Outputs:
- gradient: bfloat16 [8, 64, 128, 8192], P('day', 'pair')
The draws below stay inside these ranges and needn't reach their ends.
Inputs may be any that keep to these rules, and one draw needn't show every extreme that they name: `window_of_day`: window 0 holds exactly 2 days, window 1 the other 6.
All inputs are finite; a program needn't handle non-finite values. No bound on the sum of `pair_mask` on one device may be relied on, other than what follows from the above.
Results may differ from the reference program's by a relative error of at most 0.012.
Values may be sent and summed in bfloat16 or wider, within the bound.
No kernel may reach another device: no remote copies, remote signals or barrier semaphores. Data moves between devices by JAX's collectives and lax.ppermute only.
A program may use at most 128 MiB of HBM per device.

```python
import math
import jax
import jax.numpy as jnp

B = 128
F = 4096
NBAND = 8
REACH = 2
BLOCKS = 64
DAYS = 8


def draw_window_of_day(key, part):
    order = jax.random.permutation(jax.random.fold_in(key, 17), DAYS)
    first_count = max(1, DAYS // 3)
    positions = jnp.arange(DAYS, dtype=jnp.int32)
    labels = (positions >= first_count).astype(jnp.int32)
    window_ids = jnp.zeros((DAYS,), jnp.int32).at[order].set(labels)
    return window_ids.astype(jnp.int32)


def with_ends(drawn, own_key, smallest, high):
    extent = drawn.shape
    place = [jax.random.randint(jax.random.fold_in(own_key, axis), (), 0, extent[axis]) for axis in range(len(extent))]
    drawn = drawn.at[tuple(place)].set(smallest)
    longest = extent.index(max(extent))
    place[longest] = (place[longest] + 1) % extent[longest]
    return drawn.at[tuple(place)].set(high)


def block_scale(key, extent, pieces, low, high):
    def one(position, parts):
        steps = jax.random.uniform(jax.random.fold_in(jax.random.fold_in(key, 6), position), (parts,), jnp.float32, low / len(pieces), high / len(pieces))
        return jnp.repeat(jnp.exp(steps), extent[position] // parts).reshape((-1,) + (1,) * (len(extent) - position - 1))

    level = one(*pieces[0])
    for cut in pieces[1:]:
        level = level * one(*cut)
    return level


def scatter_about(key, shape, deviation, most, split=(), kind=jnp.bfloat16):
    result = deviation * jax.random.normal(key, shape, jnp.float32)
    if split:
        result = result * block_scale(key, shape, split, -0.22, 0.18)
    return jnp.clip(result, -most, most).astype(kind)


def setup_inputs(seed: int = 0) -> dict:
    arg_keys = jax.random.split(jax.random.key(seed), 5)
    spectra = scatter_about(arg_keys[0], (DAYS, BLOCKS, B, 2 * F), 1.0, 6.0, ((0, 4), (1, 64)))
    pair_mask = with_ends((jax.random.randint(arg_keys[1], (BLOCKS, REACH), 0, 2) < 1).astype(jnp.int32), jax.random.fold_in(arg_keys[1], 1), 0, 1)
    window_of_day = draw_window_of_day(jax.random.fold_in(arg_keys[4], 71), 0)
    band_weight = jnp.clip(jnp.exp(jax.random.uniform(arg_keys[3], (NBAND,), jnp.float32, math.log(0.5), math.log(4.0))), 0.5, 4.0)
    return {"spectra": spectra, "pair_mask": pair_mask, "window_of_day": window_of_day, "band_weight": band_weight}


def reference(spectra, pair_mask, window_of_day, band_weight):
    days, blocks, stations, row_width = spectra.shape
    band_bins = row_width // (2 * NBAND)
    norm_scale = (2.0 * band_bins) ** -0.5
    fields = spectra.astype(jnp.float32).reshape(days, blocks, stations, 2, NBAND, band_bins)
    count_first = jnp.sum((window_of_day == 0).astype(jnp.float32))
    count_second = jnp.sum((window_of_day == 1).astype(jnp.float32))
    day_weight = jnp.where(window_of_day == 0, 1.0 / count_first, -1.0 / count_second).astype(jnp.float32)
    gradient = jnp.zeros(fields.shape, jnp.float32)
    block_ids = jnp.arange(blocks, dtype=jnp.int32)
    for offset in range(1, REACH + 1):
        padding = jnp.zeros((days, offset, stations, 2, NBAND, band_bins), jnp.float32)
        partner = jnp.concatenate([fields[:, offset:], padding], axis=1)
        band_power = jnp.einsum('dgicnf,dgjcnf->dgnij', fields, partner) * norm_scale
        difference = jnp.einsum('d,dgnij->gnij', day_weight, band_power)
        listed = pair_mask[:, offset - 1] * (block_ids + offset < blocks).astype(jnp.int32)
        difference = difference * listed.astype(jnp.float32)[:, None, None, None]
        weighted = (band_weight[None, :, None, None] * difference).astype(jnp.bfloat16).astype(jnp.float32)
        home_term = jnp.einsum('gnij,dgjcnf->dgicnf', weighted, partner)
        partner_term = jnp.einsum('gnij,dgicnf->dgjcnf', weighted, fields)
        moved_term = jnp.concatenate([padding, partner_term[:, :blocks - offset]], axis=1)
        gradient = gradient + home_term + moved_term
    gradient = gradient * (day_weight * norm_scale)[:, None, None, None, None, None]
    return gradient.reshape(spectra.shape).astype(jnp.bfloat16)
```

```python
import functools

import jax
import jax.numpy as jnp
from jax import lax
from jax.experimental import pallas as pl
from jax.experimental.pallas import tpu as pltpu
from jax.sharding import Mesh
from jax.sharding import PartitionSpec as P

NBAND = 8
RING = 4
TAGS = 2
RING_AXES = ("xh", "xl")
ANY = pl.BlockSpec(memory_space=pl.ANY)
SMEM = pl.BlockSpec(memory_space=pltpu.SMEM)


def ring_place():
    return lax.axis_index("xh") * 2 + lax.axis_index("xl")


def pack(spectra, tag):
    days, _, stations, width = spectra.shape
    bins = width // (2 * NBAND)

    def kernel(x_ref, *refs):
        outs, (held, in_sem, out_sem) = refs[:RING], refs[RING:]
        place = ring_place()
        loads, stores = [], []
        for k in range(RING):
            band = RING * tag + (place ^ k)
            for c in range(2):
                start = pl.multiple_of(c * NBAND * bins + band * bins, bins)
                load = pltpu.make_async_copy(
                    x_ref.at[:, 0, :, pl.ds(start, bins)],
                    held.at[k, :, :, pl.ds(c * bins, bins)],
                    in_sem.at[k, c],
                )
                load.start()
                loads.append(load)
        for k in range(RING):
            loads[2 * k].wait()
            loads[2 * k + 1].wait()
            store = pltpu.make_async_copy(held.at[k], outs[k], out_sem.at[k])
            store.start()
            stores.append(store)
        for store in stores:
            store.wait()

    piece = jax.ShapeDtypeStruct((days, stations, 2 * bins), spectra.dtype)
    return pl.pallas_call(
        kernel,
        out_shape=[piece] * RING,
        in_specs=[ANY],
        out_specs=[ANY] * RING,
        scratch_shapes=[
            pltpu.VMEM((RING,) + piece.shape, spectra.dtype),
            pltpu.SemaphoreType.DMA((RING, 2)),
            pltpu.SemaphoreType.DMA((RING,)),
        ],
        compiler_params=pltpu.CompilerParams(vmem_limit_bytes=8 << 20),
        cost_estimate=pl.CostEstimate(flops=0, transcendentals=0, bytes_accessed=4 << 20),
        name=f"pack{tag}",
    )(spectra)


def unpack(pieces, tag, shape, into=None):
    days, _, stations, width = shape
    bins = width // (2 * NBAND)
    dtype = pieces[0].dtype
    given = list(pieces) + ([] if into is None else [into])

    def kernel(*refs):
        ins, out_ref = refs[:RING], refs[len(given)]
        held, in_sem, out_sem = refs[len(given) + 1 :]
        place = ring_place()
        loads, stores = [], []
        for k in range(RING):
            load = pltpu.make_async_copy(ins[k], held.at[k], in_sem.at[k])
            load.start()
            loads.append(load)
        for k in range(RING):
            loads[k].wait()
            band = RING * tag + (place ^ k)
            for c in range(2):
                start = pl.multiple_of(c * NBAND * bins + band * bins, bins)
                store = pltpu.make_async_copy(
                    held.at[k, :, :, pl.ds(c * bins, bins)],
                    out_ref.at[:, 0, :, pl.ds(start, bins)],
                    out_sem.at[k, c],
                )
                store.start()
                stores.append(store)
        for store in stores:
            store.wait()

    return pl.pallas_call(
        kernel,
        out_shape=jax.ShapeDtypeStruct(shape, dtype),
        in_specs=[ANY] * len(given),
        out_specs=ANY,
        scratch_shapes=[
            pltpu.VMEM((RING,) + pieces[0].shape, dtype),
            pltpu.SemaphoreType.DMA((RING,)),
            pltpu.SemaphoreType.DMA((RING, 2)),
        ],
        input_output_aliases={} if into is None else {RING: 0},
        compiler_params=pltpu.CompilerParams(vmem_limit_bytes=8 << 20),
        cost_estimate=pl.CostEstimate(flops=0, transcendentals=0, bytes_accessed=4 << 20),
        name=f"unpack{tag}",
    )(*given)


def stacked(refs, q, at):
    return jnp.concatenate([refs[q][at], refs[q + 2][at]], axis=0)


def dot_nt(a, b):
    return lax.dot_general(a, b, (((1,), (1,)), ((), ())), preferred_element_type=jnp.float32)


def dot_nn(a, b):
    return lax.dot_general(a, b, (((1,), (0,)), ((), ())), preferred_element_type=jnp.float32)


def powers(day_weight, here, above, below):
    days, stations, width = here[0].shape
    cols = width // 2
    wide = 2 * stations

    def kernel(w_ref, *refs):
        s, d, u = refs[:RING], refs[RING : 2 * RING], refs[2 * RING : 3 * RING]
        side, up, down = refs[3 * RING :]
        day = pl.program_id(0)

        @pl.when((day == 0) & (pl.program_id(1) == 0))
        def _():
            side[...] = jnp.zeros_like(side)
            up[...] = jnp.zeros_like(up)
            down[...] = jnp.zeros_like(down)

        for q in range(2):
            w = w_ref[q, day]
            mine = stacked(s, q, 0)
            side[...] += w * dot_nt(s[q][0], s[q + 2][0])
            up[...] += w * dot_nt(mine, stacked(d, q, 0))
            down[...] += w * dot_nt(mine, stacked(u, q, 0))

    block = pl.BlockSpec((1, stations, cols), lambda i, j: (i, 0, j))
    whole = lambda i, j: (0, 0)
    flops = 2 * wide * width * 2 * days * (2 * wide + stations // 2)
    return pl.pallas_call(
        kernel,
        grid=(days, 2),
        out_shape=[
            jax.ShapeDtypeStruct((stations, stations), jnp.float32),
            jax.ShapeDtypeStruct((wide, wide), jnp.float32),
            jax.ShapeDtypeStruct((wide, wide), jnp.float32),
        ],
        in_specs=[SMEM] + [block] * (3 * RING),
        out_specs=[
            pl.BlockSpec((stations, stations), whole),
            pl.BlockSpec((wide, wide), whole),
            pl.BlockSpec((wide, wide), whole),
        ],
        compiler_params=pltpu.CompilerParams(vmem_limit_bytes=32 << 20),
        cost_estimate=pl.CostEstimate(flops=flops, transcendentals=0, bytes_accessed=7 << 20),
        name="powers",
    )(day_weight, *here, *above, *below)


def gradients(scale, coef, mine, other, here, above, below):
    days, stations, width = here[0].shape
    cols = width // 2
    wide = 2 * stations

    def kernel(w_ref, c_ref, *refs):
        sums, refs = refs[:6], refs[6:]
        s, d, u = refs[:RING], refs[RING : 2 * RING], refs[2 * RING : 3 * RING]
        outs, (flat,) = refs[3 * RING : 4 * RING], refs[4 * RING :]
        day = pl.program_id(0)
        top, bottom = pl.ds(0, stations), pl.ds(stations, stations)

        @pl.when((day == 0) & (pl.program_id(1) == 0))
        def _():
            cross = (c_ref[0] * (sums[0][...] + sums[3][...])).astype(flat.dtype)
            flat[0, top, top] = jnp.zeros_like(cross)
            flat[0, bottom, bottom] = jnp.zeros_like(cross)
            flat[0, top, bottom] = cross
            flat[0, bottom, top] = (c_ref[0] * (sums[0][...] + sums[3][...])).T.astype(flat.dtype)
            for way in (1, 2):
                for i, rows in enumerate((top, bottom)):
                    for j, columns in enumerate((top, bottom)):
                        total = sums[way][rows, columns] + sums[way + 3][rows, columns]
                        flat[way, rows, columns] = (c_ref[4 * way - 3 + 2 * i + j] * total).astype(flat.dtype)

        for q in range(2):
            total = dot_nn(flat[0], stacked(s, q, 0))
            total += dot_nn(flat[1], stacked(d, q, 0))
            total += dot_nn(flat[2], stacked(u, q, 0))
            total = (w_ref[q, day] * total).astype(outs[0].dtype)
            outs[q][0] = total[:stations]
            outs[q + 2][0] = total[stations:]

    block = pl.BlockSpec((1, stations, cols), lambda i, j: (i, 0, j))
    sum_specs = [pl.BlockSpec(a.shape, lambda i, j: (0, 0)) for a in mine]
    flops = 2 * wide * width * 2 * days * 3 * wide
    return pl.pallas_call(
        kernel,
        grid=(days, 2),
        out_shape=[jax.ShapeDtypeStruct(here[0].shape, here[0].dtype)] * RING,
        in_specs=[SMEM, SMEM] + sum_specs * 2 + [block] * (3 * RING),
        out_specs=[block] * RING,
        scratch_shapes=[pltpu.VMEM((3, wide, wide), jnp.bfloat16)],
        compiler_params=pltpu.CompilerParams(vmem_limit_bytes=32 << 20),
        cost_estimate=pl.CostEstimate(flops=flops, transcendentals=0, bytes_accessed=9 << 20),
        name="gradients",
    )(scale, coef, *mine, *other, *here, *above, *below)


def ring_swap(x, k):
    return lax.ppermute(x, RING_AXES, [(i, i ^ k) for i in range(RING)])


def move_up(x, columns):
    return lax.ppermute(x, "h", [(i, i + 1) for i in range(columns - 1)])


def move_down(x, columns):
    return lax.ppermute(x, "h", [(i + 1, i) for i in range(columns - 1)])


def core_swap(x):
    return lax.ppermute(x, "c", [(0, 1), (1, 0)])


def coefficients(pair_mask, columns):
    own = pair_mask[0].astype(jnp.float32)
    listed = jnp.stack([own, ring_swap(own, 2)])
    before = move_up(listed, columns)
    first = lax.axis_index("xh") == 0
    zero = jnp.zeros((), jnp.float32)
    return jnp.stack(
        [
            jnp.where(first, listed[0, 0], listed[1, 0]),
            listed[0, 1],
            jnp.where(first, zero, listed[0, 0]),
            jnp.where(first, listed[1, 0], zero),
            listed[1, 1],
            before[0, 1],
            jnp.where(first, before[1, 0], zero),
            jnp.where(first, zero, before[0, 0]),
            before[1, 1],
        ]
    )


def shards(spectra, pair_mask, window_of_day, band_weight):
    days, _, stations, width = spectra.shape
    columns = lax.axis_size("h")
    norm_scale = (2.0 * (width // (2 * NBAND))) ** (-0.5)
    count_first = jnp.sum((window_of_day == 0).astype(jnp.float32))
    count_second = jnp.sum((window_of_day == 1).astype(jnp.float32))
    all_weights = jnp.where(window_of_day == 0, 1.0 / count_first, -1.0 / count_second)
    by_device = all_weights.reshape(2, 2, days)
    half = lax.axis_index("xl")
    on_core = lax.dynamic_index_in_dim(by_device, lax.axis_index("c"), 1, keepdims=False)
    day_weight = jnp.where(half == 0, on_core, on_core[::-1])

    packed = [pack(spectra, tag) for tag in range(TAGS)]
    mask = coefficients(pair_mask, columns)
    here = [[p[0]] + [ring_swap(p[k], k) for k in range(1, RING)] for p in packed]
    above = [[move_down(piece, columns) for piece in pieces] for pieces in here]
    below = [[move_up(piece, columns) for piece in pieces] for pieces in here]
    out = None
    for tag in range(TAGS):
        mine = powers(day_weight, here[tag], above[tag], below[tag])
        other = [core_swap(m) for m in mine]
        weight = lax.dynamic_index_in_dim(band_weight, RING * tag + ring_place(), 0, keepdims=False)
        grads = gradients(
            day_weight * norm_scale,
            mask * (weight * norm_scale),
            mine,
            other,
            here[tag],
            above[tag],
            below[tag],
        )
        moved = [grads[0]] + [ring_swap(grads[k], k) for k in range(1, RING)]
        out = unpack(moved, tag, spectra.shape, out)
    return out


def solution(mesh):
    columns = mesh.shape["pair"] // 2
    fine = Mesh(mesh.devices.reshape(columns, 2, 2, 2), ("h", "xh", "xl", "c"))
    return jax.shard_map(
        shards,
        mesh=fine,
        in_specs=(P(("xl", "c"), ("h", "xh"), None, None), P(("h", "xh"), None), P(), P()),
        out_specs=P(("xl", "c"), ("h", "xh"), None, None),
        check_vma=False,
    )
```

```python
import jax
import jax.numpy as jnp
from jax import lax
from jax.experimental import pallas as pl
from jax.experimental.pallas import tpu as pltpu
from jax.sharding import Mesh
from jax.sharding import PartitionSpec as P

NBAND = 8
RING = 4
TAGS = 2
MASK_ROWS = 8
SENT = (1, 3, 2)
RING_AXES = ("xh", "xl")
ANY = pl.BlockSpec(memory_space=pl.ANY)
SMEM = pl.BlockSpec(memory_space=pltpu.SMEM)


def call(kernel, vmem=16 << 20, **how):
    return pl.pallas_call(kernel, compiler_params=pltpu.CompilerParams(vmem_limit_bytes=vmem), **how)


def ring_place():
    return lax.axis_index("xh") * 2 + lax.axis_index("xl")


def column_start(tag, k, c, bins):
    band = RING * tag + (ring_place() ^ k)
    return pl.multiple_of(c * NBAND * bins + band * bins, bins)


def pack(spectra, pair_mask, wanted):
    days, _, stations, width = spectra.shape
    bins = width // (2 * NBAND)
    rows = days * stations
    count = sum(len(pieces) for pieces, _ in wanted)
    masked = any(mask for _, mask in wanted)

    def kernel(x_ref, m_ref, *refs):
        outs = refs[: len(wanted)]
        held, slab, in_sem, out_sem, slab_sem = refs[len(wanted) :]
        loads, stores, at = [], [], 0
        for pieces, _ in wanted:
            for tag, k in pieces:
                for c in range(2):
                    for d in range(days):
                        load = pltpu.make_async_copy(
                            x_ref.at[d, 0, :, pl.ds(column_start(tag, k, c, bins), bins)],
                            held.at[at, pl.ds(d * stations, stations), pl.ds(c * bins, bins)],
                            in_sem.at[at, c, d],
                        )
                        load.start()
                        loads.append(load)
                at += 1
        if masked:
            row = lax.broadcasted_iota(jnp.int32, slab.shape, 0)
            first, second = m_ref[0, 0].astype(jnp.float32), m_ref[0, 1].astype(jnp.float32)
            value = jnp.where(row == 0, first, jnp.where(row == 1, second, 0.0))
            slab[...] = value.astype(slab.dtype)
        at = 0
        for out, (pieces, mask) in zip(outs, wanted):
            for i in range(len(pieces)):
                for load in loads[2 * days * at : 2 * days * (at + 1)]:
                    load.wait()
                store = pltpu.make_async_copy(held.at[at], out.at[pl.ds(i * rows, rows), :], out_sem.at[at])
                store.start()
                stores.append(store)
                at += 1
        for j, (out, (pieces, mask)) in enumerate(zip(outs, wanted)):
            if mask:
                store = pltpu.make_async_copy(
                    slab, out.at[pl.ds(len(pieces) * rows, MASK_ROWS), :], slab_sem.at[j]
                )
                store.start()
                stores.append(store)
        for store in stores:
            store.wait()

    return call(
        kernel,
        out_shape=[
            jax.ShapeDtypeStruct((len(pieces) * rows + MASK_ROWS * mask, 2 * bins), spectra.dtype)
            for pieces, mask in wanted
        ],
        in_specs=[ANY, SMEM],
        out_specs=[ANY] * len(wanted),
        scratch_shapes=[
            pltpu.VMEM((count, rows, 2 * bins), spectra.dtype),
            pltpu.VMEM((MASK_ROWS, 2 * bins), spectra.dtype),
            pltpu.SemaphoreType.DMA((count, 2, days)),
            pltpu.SemaphoreType.DMA((count,)),
            pltpu.SemaphoreType.DMA((len(wanted),)),
        ],
        cost_estimate=pl.CostEstimate(flops=0, transcendentals=0, bytes_accessed=count << 20),
        vmem=60 << 20,
    )(spectra, pair_mask)


def join(pieces):
    rows = [p.shape[0] for p in pieces]
    starts = [sum(rows[:i]) for i in range(len(rows))]
    width, dtype = pieces[0].shape[1], pieces[0].dtype

    def kernel(*refs):
        ins, out, held, in_sem, out_sem = refs[:-4], *refs[-4:]
        spans = [pl.ds(start, n) for start, n in zip(starts, rows)]
        loads = [pltpu.make_async_copy(r, held.at[at, :], in_sem.at[i]) for i, (r, at) in enumerate(zip(ins, spans))]
        stores = [pltpu.make_async_copy(held.at[at, :], out.at[at, :], out_sem.at[i]) for i, at in enumerate(spans)]
        for load in loads:
            load.start()
        for load, store in zip(loads, stores):
            load.wait()
            store.start()
        for store in stores:
            store.wait()

    return call(
        kernel,
        out_shape=jax.ShapeDtypeStruct((sum(rows), width), dtype),
        in_specs=[ANY] * len(rows),
        out_specs=ANY,
        scratch_shapes=[
            pltpu.VMEM((sum(rows), width), dtype),
            pltpu.SemaphoreType.DMA((len(rows),)),
            pltpu.SemaphoreType.DMA((len(rows),)),
        ],
        cost_estimate=pl.CostEstimate(flops=0, transcendentals=0, bytes_accessed=3 << 20),
    )(*pieces)


def unpack(pieces, tag, shape, into=None):
    days, _, stations, width = shape
    bins = width // (2 * NBAND)
    dtype = pieces[0].dtype
    given = list(pieces) + ([] if into is None else [into])

    def kernel(*refs):
        ins, out_ref = refs[:RING], refs[len(given)]
        held, in_sem, out_sem = refs[len(given) + 1 :]
        loads, stores = [], []
        for k in range(RING):
            load = pltpu.make_async_copy(ins[k], held.at[k], in_sem.at[k])
            load.start()
            loads.append(load)
        for k in range(RING):
            loads[k].wait()
            for c in range(2):
                for d in range(days):
                    store = pltpu.make_async_copy(
                        held.at[k, pl.ds(d * stations, stations), pl.ds(c * bins, bins)],
                        out_ref.at[d, 0, :, pl.ds(column_start(tag, k, c, bins), bins)],
                        out_sem.at[k, c, d],
                    )
                    store.start()
                    stores.append(store)
        for store in stores:
            store.wait()

    return call(
        kernel,
        out_shape=jax.ShapeDtypeStruct(shape, dtype),
        in_specs=[ANY] * len(given),
        out_specs=ANY,
        scratch_shapes=[
            pltpu.VMEM((RING,) + pieces[0].shape, dtype),
            pltpu.SemaphoreType.DMA((RING,)),
            pltpu.SemaphoreType.DMA((RING, 2, days)),
        ],
        input_output_aliases={} if into is None else {RING: 0},
        cost_estimate=pl.CostEstimate(flops=0, transcendentals=0, bytes_accessed=4 << 20),
    )(*given)


def dot_nt(a, b):
    return lax.dot_general(a, b, (((1,), (1,)), ((), ())), preferred_element_type=jnp.float32)


def dot_nn(a, b):
    return lax.dot_general(a, b, (((1,), (0,)), ((), ())), preferred_element_type=jnp.float32)


def slot_blocks(sources, k, rows, cols):
    array, place = sources[k]
    return array, pl.BlockSpec((rows, cols), lambda j: (place, j))


def mask_blocks(array, width):
    place = array.shape[0] // MASK_ROWS - 1
    return array, pl.BlockSpec((MASK_ROWS, width), lambda j: (place, 0))


def stacked(tiles, n, day, stations):
    rows = pl.ds(day * stations, stations)
    return jnp.concatenate([tiles[n][rows, :], tiles[n + 1][rows, :]], axis=0)


def powers(day_weight, q, days, stations, sources, before=None):
    width = sources[0][0][0].shape[1]
    steps = 2
    cols = width // steps
    wide = 2 * stations
    extra = [] if before is None else [before]

    def kernel(w_ref, *refs):
        tiles, out = refs[:6], refs[-1]

        @pl.when(pl.program_id(0) == 0)
        def _():
            out[...] = jnp.zeros_like(out) if before is None else refs[6][...]

        up = down = side = 0.0
        for day in range(days):
            w = w_ref[q, day]
            mine, above, below = (stacked(tiles, n, day, stations) for n in (0, 2, 4))
            up += w * dot_nt(mine, above)
            down += w * dot_nt(mine, below)
            side += w * dot_nt(mine[:stations], mine)
        out[pl.ds(0, wide), :] += up
        out[pl.ds(wide, wide), :] += down
        out[pl.ds(2 * wide, stations), :] += side

    blocks = [slot_blocks(source, k, days * stations, cols) for source in sources for k in (q, q + 2)]
    shape = (5 * stations, wide)
    whole = pl.BlockSpec(shape, lambda j: (0, 0))
    return call(
        kernel,
        grid=(steps,),
        out_shape=jax.ShapeDtypeStruct(shape, jnp.float32),
        in_specs=[SMEM] + [spec for _, spec in blocks] + [whole] * len(extra),
        out_specs=whole,
        cost_estimate=pl.CostEstimate(
            flops=2 * wide * wide * 3 * width * days, transcendentals=0, bytes_accessed=4 << 20
        ),
    )(day_weight, *[a for a, _ in blocks], *extra)


def weigh(scale, mine, other, masks, stations):
    wide = 2 * stations

    def kernel(c_ref, p_ref, r_ref, here_a, here_b, below_a, below_b, out):
        top, bottom = pl.ds(0, stations), pl.ds(stations, stations)
        scale = c_ref[0]
        first = (lax.axis_index("xh") == 0).astype(jnp.float32)
        ha, hb, ba, bb = (
            m[...].astype(jnp.float32)[:, :stations] * scale for m in (here_a, here_b, below_a, below_b)
        )
        low = first * ha[0:1] + (1.0 - first) * hb[0:1]
        total = low * (p_ref[pl.ds(2 * wide, stations), bottom] + r_ref[pl.ds(2 * wide, stations), bottom])
        blank = jnp.zeros((stations, stations), out.dtype)
        out[0, top, top] = blank
        out[0, bottom, bottom] = blank
        out[0, top, bottom] = total.astype(out.dtype)
        out[0, bottom, top] = total.T.astype(out.dtype)
        column = lax.axis_index("h")
        has_next = (column < lax.axis_size("h") - 1).astype(jnp.float32)
        has_previous = (column > 0).astype(jnp.float32)
        ha, hb, ba, bb = has_next * ha, has_next * hb, has_previous * ba, has_previous * bb
        up = ((ha[1:2], (1.0 - first) * ha[0:1]), (first * hb[0:1], hb[1:2]))
        down = ((ba[1:2], first * bb[0:1]), ((1.0 - first) * ba[0:1], bb[1:2]))
        for way, factors in ((1, up), (2, down)):
            for i, rows in enumerate((top, bottom)):
                for j, columns in enumerate((top, bottom)):
                    at = pl.ds((way - 1) * wide + i * stations, stations)
                    total = factors[i][j] * (p_ref[at, columns] + r_ref[at, columns])
                    out[way, rows, columns] = total.astype(out.dtype)

    whole = pl.BlockSpec(mine.shape, lambda j: (0, 0))
    blocks = [mask_blocks(m, wide) for m in masks]
    return call(
        kernel,
        grid=(1,),
        out_shape=jax.ShapeDtypeStruct((3, wide, wide), jnp.bfloat16),
        in_specs=[SMEM, whole, whole] + [spec for _, spec in blocks],
        out_specs=pl.BlockSpec((3, wide, wide), lambda j: (0, 0, 0)),
        cost_estimate=pl.CostEstimate(flops=0, transcendentals=0, bytes_accessed=2 << 20),
    )(scale, mine, other, *[a for a, _ in blocks])


def gradients(day_scale, weighted, q, days, stations, sources):
    own = sources[0][0][0]
    width = own.shape[1]
    rows = days * stations
    steps = 2
    cols = width // steps
    wide = 2 * stations

    def kernel(w_ref, m_ref, *refs):
        tiles, outs = refs[:6], refs[6:]
        for day in range(days):
            mine, above, below = (stacked(tiles, n, day, stations) for n in (0, 2, 4))
            total = dot_nn(m_ref[0], mine) + dot_nn(m_ref[1], above) + dot_nn(m_ref[2], below)
            total = (w_ref[q, day] * total).astype(outs[0].dtype)
            outs[0][pl.ds(day * stations, stations), :] = total[:stations]
            outs[1][pl.ds(day * stations, stations), :] = total[stations:]

    blocks = [slot_blocks(source, k, rows, cols) for source in sources for k in (q, q + 2)]
    piece = pl.BlockSpec((rows, cols), lambda j: (0, j))
    return call(
        kernel,
        grid=(steps,),
        out_shape=[jax.ShapeDtypeStruct((rows, width), own.dtype)] * 2,
        in_specs=[SMEM, pl.BlockSpec(weighted.shape, lambda j: (0, 0, 0))] + [spec for _, spec in blocks],
        out_specs=[piece] * 2,
        cost_estimate=pl.CostEstimate(
            flops=2 * wide * wide * 3 * width * days, transcendentals=0, bytes_accessed=5 << 20
        ),
    )(day_scale, weighted, *[a for a, _ in blocks])


def ring_swap(x, k):
    return lax.ppermute(x, RING_AXES, [(i, i ^ k) for i in range(RING)])


def move_up(x, columns):
    return lax.ppermute(x, "h", [(i, (i + 1) % columns) for i in range(columns)])


def move_down(x, columns):
    return lax.ppermute(x, "h", [((i + 1) % columns, i) for i in range(columns)])


def core_swap(x):
    return lax.ppermute(x, "c", [(0, 1), (1, 0)])


def shards(spectra, pair_mask, window_of_day, band_weight):
    days, _, stations, width = spectra.shape
    columns = lax.axis_size("h")
    norm_scale = (2.0 * (width // (2 * NBAND))) ** (-0.5)
    count_first = jnp.sum((window_of_day == 0).astype(jnp.float32))
    count_second = jnp.sum((window_of_day == 1).astype(jnp.float32))
    all_weights = jnp.where(window_of_day == 0, 1.0 / count_first, -1.0 / count_second)
    by_device = all_weights.reshape(2, 2, days)
    on_core = lax.dynamic_index_in_dim(by_device, lax.axis_index("c"), 1, keepdims=False)
    day_weight = jnp.where(lax.axis_index("xl") == 0, on_core, on_core[::-1])
    day_scale = day_weight * norm_scale
    weights = band_weight.reshape(TAGS, RING) * norm_scale

    (own,) = pack(spectra, pair_mask, [(((0, 0), (1, 0)), True)])
    first = pack(spectra, pair_mask, [(((0, k),), k == 2) for k in SENT])
    second = pack(spectra, pair_mask, [(((1, k),), False) for k in SENT])
    here_own = [own, move_down(own, columns), move_up(own, columns)]
    sources, singles = [], []
    for tag, sent in enumerate((first, second)):
        came = [ring_swap(piece, k) for k, piece in zip(SENT, sent)]
        pair, single = join(came[:2]), came[2]
        pairs = [pair, move_down(pair, columns), move_up(pair, columns)]
        single = [single, move_down(single, columns), move_up(single, columns)]
        sources.append([((o, tag), (p, 0), (s, 0), (p, 1)) for o, p, s in zip(here_own, pairs, single)])
        singles.append(single)
    masks = [own, singles[0][0], here_own[2], singles[0][2]]
    out = None
    for tag in range(TAGS):
        mine = powers(day_weight, 1, days, stations, sources[tag])
        mine = powers(day_weight, 0, days, stations, sources[tag], mine)
        other = core_swap(mine)
        scale = lax.dynamic_index_in_dim(weights[tag], ring_place(), 0)
        weighted = weigh(scale, mine, other, masks, stations)
        grads = [None] * RING
        for q in (1, 0):
            grads[q], grads[q + 2] = gradients(day_scale, weighted, q, days, stations, sources[tag])
        moved = [grads[0]] + [ring_swap(grads[k], k) for k in range(1, RING)]
        out = unpack(moved, tag, spectra.shape, out)
    return out


def solution(mesh):
    columns = mesh.shape["pair"] // 2
    fine = Mesh(mesh.devices.reshape(columns, 2, 2, 2), ("h", "xh", "xl", "c"))
    return jax.shard_map(
        shards,
        mesh=fine,
        in_specs=(P(("xl", "c"), ("h", "xh"), None, None), P(("h", "xh"), None), P(), P()),
        out_specs=P(("xl", "c"), ("h", "xh"), None, None),
        check_vma=False,
    )
```

```python
import jax
import jax.numpy as jnp
from jax import lax
from jax.experimental import pallas as pl
from jax.experimental.pallas import tpu as pltpu
from jax.sharding import Mesh
from jax.sharding import PartitionSpec as P

NBAND = 8
RING = 4
MASK_ROWS = 8
SENT = (1, 3, 2)
RING_AXES = ("xh", "xl")
ANY = pl.BlockSpec(memory_space=pl.ANY)
SMEM = pl.BlockSpec(memory_space=pltpu.SMEM)


def call(kernel, vmem=16 << 20, **how):
    return pl.pallas_call(kernel, compiler_params=pltpu.CompilerParams(vmem_limit_bytes=vmem), **how)


def ring_place():
    return lax.axis_index("xh") * 2 + lax.axis_index("xl")


def column_start(tag, k, c, bins):
    band = RING * tag + (ring_place() ^ k)
    return pl.multiple_of(c * NBAND * bins + band * bins, bins)


def pack(spectra, pair_mask, wanted):
    days, _, stations, width = spectra.shape
    bins = width // (2 * NBAND)
    rows = days * stations
    count = sum(len(pieces) for pieces, _ in wanted)
    masked = any(mask for _, mask in wanted)

    def kernel(x_ref, m_ref, *refs):
        outs = refs[: len(wanted)]
        held, slab, in_sem, out_sem, slab_sem = refs[len(wanted) :]
        loads, stores, at = [], [], 0
        for pieces, _ in wanted:
            for tag, k in pieces:
                for c in range(2):
                    for d in range(days):
                        load = pltpu.make_async_copy(
                            x_ref.at[d, 0, :, pl.ds(column_start(tag, k, c, bins), bins)],
                            held.at[at, pl.ds(d * stations, stations), pl.ds(c * bins, bins)],
                            in_sem.at[at, c, d],
                        )
                        load.start()
                        loads.append(load)
                at += 1
        if masked:
            row = lax.broadcasted_iota(jnp.int32, slab.shape, 0)
            first, second = m_ref[0, 0].astype(jnp.float32), m_ref[0, 1].astype(jnp.float32)
            value = jnp.where(row == 0, first, jnp.where(row == 1, second, 0.0))
            slab[...] = value.astype(slab.dtype)
        at = 0
        for out, (pieces, mask) in zip(outs, wanted):
            for i in range(len(pieces)):
                for load in loads[2 * days * at : 2 * days * (at + 1)]:
                    load.wait()
                store = pltpu.make_async_copy(held.at[at], out.at[pl.ds(i * rows, rows), :], out_sem.at[at])
                store.start()
                stores.append(store)
                at += 1
        for j, (out, (pieces, mask)) in enumerate(zip(outs, wanted)):
            if mask:
                store = pltpu.make_async_copy(
                    slab, out.at[pl.ds(len(pieces) * rows, MASK_ROWS), :], slab_sem.at[j]
                )
                store.start()
                stores.append(store)
        for store in stores:
            store.wait()

    return call(
        kernel,
        out_shape=[
            jax.ShapeDtypeStruct((len(pieces) * rows + MASK_ROWS * mask, 2 * bins), spectra.dtype)
            for pieces, mask in wanted
        ],
        in_specs=[ANY, SMEM],
        out_specs=[ANY] * len(wanted),
        scratch_shapes=[
            pltpu.VMEM((count, rows, 2 * bins), spectra.dtype),
            pltpu.VMEM((MASK_ROWS, 2 * bins), spectra.dtype),
            pltpu.SemaphoreType.DMA((count, 2, days)),
            pltpu.SemaphoreType.DMA((count,)),
            pltpu.SemaphoreType.DMA((len(wanted),)),
        ],
        cost_estimate=pl.CostEstimate(flops=0, transcendentals=0, bytes_accessed=count << 20),
        vmem=60 << 20,
    )(spectra, pair_mask)


def join(pieces):
    rows = [p.shape[0] for p in pieces]
    starts = [sum(rows[:i]) for i in range(len(rows))]
    width, dtype = pieces[0].shape[1], pieces[0].dtype

    def kernel(*refs):
        ins, out, held, in_sem, out_sem = refs[:-4], *refs[-4:]
        spans = [pl.ds(start, n) for start, n in zip(starts, rows)]
        loads = [pltpu.make_async_copy(r, held.at[at, :], in_sem.at[i]) for i, (r, at) in enumerate(zip(ins, spans))]
        stores = [pltpu.make_async_copy(held.at[at, :], out.at[at, :], out_sem.at[i]) for i, at in enumerate(spans)]
        for load in loads:
            load.start()
        for load, store in zip(loads, stores):
            load.wait()
            store.start()
        for store in stores:
            store.wait()

    return call(
        kernel,
        out_shape=jax.ShapeDtypeStruct((sum(rows), width), dtype),
        in_specs=[ANY] * len(rows),
        out_specs=ANY,
        scratch_shapes=[
            pltpu.VMEM((sum(rows), width), dtype),
            pltpu.SemaphoreType.DMA((len(rows),)),
            pltpu.SemaphoreType.DMA((len(rows),)),
        ],
        cost_estimate=pl.CostEstimate(flops=0, transcendentals=0, bytes_accessed=3 << 20),
    )(*pieces)


def unpack(pieces, tag, shape, into=None):
    days, _, stations, width = shape
    bins = width // (2 * NBAND)
    slots, arrays = list(pieces), list(pieces.values())
    count, dtype = len(slots), arrays[0].dtype
    given = arrays + ([] if into is None else [into])

    def kernel(*refs):
        ins, out_ref = refs[:count], refs[len(given)]
        held, in_sem, out_sem = refs[len(given) + 1 :]
        loads, stores = [], []
        for n in range(count):
            load = pltpu.make_async_copy(ins[n], held.at[n], in_sem.at[n])
            load.start()
            loads.append(load)
        for n, k in enumerate(slots):
            loads[n].wait()
            for c in range(2):
                for d in range(days):
                    store = pltpu.make_async_copy(
                        held.at[n, pl.ds(d * stations, stations), pl.ds(c * bins, bins)],
                        out_ref.at[d, 0, :, pl.ds(column_start(tag, k, c, bins), bins)],
                        out_sem.at[n, c, d],
                    )
                    store.start()
                    stores.append(store)
        for store in stores:
            store.wait()

    return call(
        kernel,
        out_shape=jax.ShapeDtypeStruct(shape, dtype),
        in_specs=[ANY] * len(given),
        out_specs=ANY,
        scratch_shapes=[
            pltpu.VMEM((count,) + arrays[0].shape, dtype),
            pltpu.SemaphoreType.DMA((count,)),
            pltpu.SemaphoreType.DMA((count, 2, days)),
        ],
        input_output_aliases={} if into is None else {count: 0},
        cost_estimate=pl.CostEstimate(flops=0, transcendentals=0, bytes_accessed=count << 20),
    )(*given)


def dot_nt(a, b):
    return lax.dot_general(a, b, (((1,), (1,)), ((), ())), preferred_element_type=jnp.float32)


def dot_nn(a, b):
    return lax.dot_general(a, b, (((1,), (0,)), ((), ())), preferred_element_type=jnp.float32)


def slot_blocks(sources, k, rows, cols):
    array, place = sources[k]
    return array, pl.BlockSpec((rows, cols), lambda j: (place, j))


def mask_blocks(array, width):
    place = array.shape[0] // MASK_ROWS - 1
    return array, pl.BlockSpec((MASK_ROWS, width), lambda j: (place, 0))


def stacked(tiles, n, day, stations):
    rows = pl.ds(day * stations, stations)
    return jnp.concatenate([tiles[n][rows, :], tiles[n + 1][rows, :]], axis=0)


def powers(day_weight, q, days, stations, sources, before=None):
    width = sources[0][0][0].shape[1]
    steps = 2
    cols = width // steps
    wide = 2 * stations
    extra = [] if before is None else [before]

    def kernel(w_ref, *refs):
        tiles, out = refs[:6], refs[-1]

        @pl.when(pl.program_id(0) == 0)
        def _():
            out[...] = jnp.zeros_like(out) if before is None else refs[6][...]

        up = down = side = 0.0
        for day in range(days):
            w = w_ref[q, day]
            mine, above, below = (stacked(tiles, n, day, stations) for n in (0, 2, 4))
            up += w * dot_nt(mine, above)
            down += w * dot_nt(mine, below)
            side += w * dot_nt(mine[:stations], mine)
        out[pl.ds(0, wide), :] += up
        out[pl.ds(wide, wide), :] += down
        out[pl.ds(2 * wide, stations), :] += side

    blocks = [slot_blocks(source, k, days * stations, cols) for source in sources for k in (q, q + 2)]
    shape = (5 * stations, wide)
    whole = pl.BlockSpec(shape, lambda j: (0, 0))
    return call(
        kernel,
        grid=(steps,),
        out_shape=jax.ShapeDtypeStruct(shape, jnp.float32),
        in_specs=[SMEM] + [spec for _, spec in blocks] + [whole] * len(extra),
        out_specs=whole,
        cost_estimate=pl.CostEstimate(
            flops=2 * wide * wide * 3 * width * days, transcendentals=0, bytes_accessed=4 << 20
        ),
    )(day_weight, *[a for a, _ in blocks], *extra)


def weigh(tag, band_weight, norm_scale, mine, other, masks, stations):
    wide = 2 * stations

    def kernel(c_ref, p_ref, r_ref, here_a, here_b, below_a, below_b, out):
        top, bottom = pl.ds(0, stations), pl.ds(stations, stations)
        scale = c_ref[RING * tag + ring_place()] * norm_scale
        first = (lax.axis_index("xh") == 0).astype(jnp.float32)
        ha, hb, ba, bb = (
            m[...].astype(jnp.float32)[:, :stations] * scale for m in (here_a, here_b, below_a, below_b)
        )
        low = first * ha[0:1] + (1.0 - first) * hb[0:1]
        total = low * (p_ref[pl.ds(2 * wide, stations), bottom] + r_ref[pl.ds(2 * wide, stations), bottom])
        blank = jnp.zeros((stations, stations), out.dtype)
        out[0, top, top] = blank
        out[0, bottom, bottom] = blank
        out[0, top, bottom] = total.astype(out.dtype)
        out[0, bottom, top] = total.T.astype(out.dtype)
        column = lax.axis_index("h")
        has_next = (column < lax.axis_size("h") - 1).astype(jnp.float32)
        has_previous = (column > 0).astype(jnp.float32)
        ha, hb, ba, bb = has_next * ha, has_next * hb, has_previous * ba, has_previous * bb
        up = ((ha[1:2], (1.0 - first) * ha[0:1]), (first * hb[0:1], hb[1:2]))
        down = ((ba[1:2], first * bb[0:1]), ((1.0 - first) * ba[0:1], bb[1:2]))
        for way, factors in ((1, up), (2, down)):
            for i, rows in enumerate((top, bottom)):
                for j, columns in enumerate((top, bottom)):
                    at = pl.ds((way - 1) * wide + i * stations, stations)
                    total = factors[i][j] * (p_ref[at, columns] + r_ref[at, columns])
                    out[way, rows, columns] = total.astype(out.dtype)

    whole = pl.BlockSpec(mine.shape, lambda j: (0, 0))
    blocks = [mask_blocks(m, wide) for m in masks]
    return call(
        kernel,
        grid=(1,),
        out_shape=jax.ShapeDtypeStruct((3, wide, wide), jnp.bfloat16),
        in_specs=[SMEM, whole, whole] + [spec for _, spec in blocks],
        out_specs=pl.BlockSpec((3, wide, wide), lambda j: (0, 0, 0)),
        cost_estimate=pl.CostEstimate(flops=0, transcendentals=0, bytes_accessed=2 << 20),
    )(band_weight, mine, other, *[a for a, _ in blocks])


def gradients(day_scale, weighted, q, days, stations, sources):
    own = sources[0][0][0]
    width = own.shape[1]
    rows = days * stations
    steps = 2
    cols = width // steps
    wide = 2 * stations

    def kernel(w_ref, m_ref, *refs):
        tiles, outs = refs[:6], refs[6:]
        for day in range(days):
            mine, above, below = (stacked(tiles, n, day, stations) for n in (0, 2, 4))
            total = dot_nn(m_ref[0], mine) + dot_nn(m_ref[1], above) + dot_nn(m_ref[2], below)
            total = (w_ref[q, day] * total).astype(outs[0].dtype)
            outs[0][pl.ds(day * stations, stations), :] = total[:stations]
            outs[1][pl.ds(day * stations, stations), :] = total[stations:]

    blocks = [slot_blocks(source, k, rows, cols) for source in sources for k in (q, q + 2)]
    piece = pl.BlockSpec((rows, cols), lambda j: (0, j))
    return call(
        kernel,
        grid=(steps,),
        out_shape=[jax.ShapeDtypeStruct((rows, width), own.dtype)] * 2,
        in_specs=[SMEM, pl.BlockSpec(weighted.shape, lambda j: (0, 0, 0))] + [spec for _, spec in blocks],
        out_specs=[piece] * 2,
        cost_estimate=pl.CostEstimate(
            flops=2 * wide * wide * 3 * width * days, transcendentals=0, bytes_accessed=5 << 20
        ),
    )(day_scale, weighted, *[a for a, _ in blocks])


def near_powers(day_weight, q, days, stations, sources, before=None):
    width = sources[0][0][0].shape[1]
    steps = 2
    cols = width // steps
    wide = 2 * stations
    extra = [] if before is None else [before]

    def kernel(w_ref, *refs):
        tiles, out = refs[:4], refs[-1]

        @pl.when(pl.program_id(0) == 0)
        def _():
            out[...] = jnp.zeros_like(out) if before is None else refs[4][...]

        across = side = 0.0
        for day in range(days):
            w = w_ref[q, day]
            mine, theirs = (stacked(tiles, n, day, stations) for n in (0, 2))
            across += w * dot_nt(mine, theirs)
            side += w * dot_nt(mine[:stations], mine)
        out[pl.ds(0, wide), :] += across
        out[pl.ds(wide, stations), :] += side

    blocks = [slot_blocks(source, k, days * stations, cols) for source in sources for k in (q, q + 2)]
    shape = (3 * stations, wide)
    whole = pl.BlockSpec(shape, lambda j: (0, 0))
    return call(
        kernel,
        grid=(steps,),
        out_shape=jax.ShapeDtypeStruct(shape, jnp.float32),
        in_specs=[SMEM] + [spec for _, spec in blocks] + [whole] * len(extra),
        out_specs=whole,
        cost_estimate=pl.CostEstimate(
            flops=2 * wide * wide * 2 * width * days, transcendentals=0, bytes_accessed=3 << 20
        ),
    )(day_weight, *[a for a, _ in blocks], *extra)


def near_weigh(tag, band_weight, norm_scale, mine, other, masks, stations):
    wide = 2 * stations

    def kernel(c_ref, p_ref, r_ref, here_a, here_b, above_a, above_b, below_a, below_b, out):
        top, bottom = pl.ds(0, stations), pl.ds(stations, stations)
        scale = c_ref[RING * tag + ring_place()] * norm_scale
        first = (lax.axis_index("xh") == 0).astype(jnp.float32)
        second = 1.0 - first
        column = lax.axis_index("h")
        has_next = (column < lax.axis_size("h") - 1).astype(jnp.float32)
        has_previous = (column > 0).astype(jnp.float32)
        ha, hb, ua, ub, la, lb = (
            m[...].astype(jnp.float32)[:, :stations] * scale
            for m in (here_a, here_b, above_a, above_b, below_a, below_b)
        )
        near_a = first * ua + second * la
        near_b = first * lb + second * ub
        ends_a = first * has_next + second * has_previous
        ends_b = first * has_previous + second * has_next
        factors = (
            (
                ends_a * (first * ha[1:2] + second * near_a[1:2]),
                ends_b * (first * near_b[0:1] + second * ha[0:1]),
            ),
            (
                ends_a * (first * hb[0:1] + second * near_a[0:1]),
                ends_b * (first * near_b[1:2] + second * hb[1:2]),
            ),
        )
        low = first * ha[0:1] + second * hb[0:1]
        total = low * (p_ref[pl.ds(wide, stations), bottom] + r_ref[pl.ds(wide, stations), bottom])
        blank = jnp.zeros((stations, stations), out.dtype)
        for way in (0, 2):
            out[way, top, top] = blank
            out[way, bottom, bottom] = blank
            out[way, top, bottom] = blank
            out[way, bottom, top] = blank
        out[0, top, bottom] = total.astype(out.dtype)
        out[0, bottom, top] = total.T.astype(out.dtype)
        for i, rows in enumerate((top, bottom)):
            for j, columns in enumerate((top, bottom)):
                total = factors[i][j] * (p_ref[rows, columns] + r_ref[rows, columns])
                out[1, rows, columns] = total.astype(out.dtype)
                if i == j:
                    out[2, rows, rows] = total.T.astype(out.dtype)

    whole = pl.BlockSpec(mine.shape, lambda j: (0, 0))
    blocks = [mask_blocks(m, wide) for m in masks]
    return call(
        kernel,
        grid=(1,),
        out_shape=jax.ShapeDtypeStruct((3, wide, wide), jnp.bfloat16),
        in_specs=[SMEM, whole, whole] + [spec for _, spec in blocks],
        out_specs=pl.BlockSpec((3, wide, wide), lambda j: (0, 0, 0)),
        cost_estimate=pl.CostEstimate(flops=0, transcendentals=0, bytes_accessed=2 << 20),
    )(band_weight, mine, other, *[a for a, _ in blocks])


def terms(weighted, days, stations, source):
    like = source[0][0]
    rows, width = days * stations, like.shape[1]
    steps = 2
    cols = width // steps

    def kernel(m_ref, *refs):
        tiles, outs = refs[:RING], refs[RING:]
        for q in (0, 1):
            pair = (tiles[q], tiles[q + 2])
            for day in range(days):
                at = pl.ds(day * stations, stations)
                total = dot_nn(m_ref[2], stacked(pair, 0, day, stations)).astype(like.dtype)
                outs[q][at, :] = total[:stations]
                outs[q + 2][at, :] = total[stations:]

    blocks = [slot_blocks(source, k, rows, cols) for k in range(RING)]
    return call(
        kernel,
        grid=(steps,),
        out_shape=[jax.ShapeDtypeStruct((rows, width), like.dtype)] * RING,
        in_specs=[pl.BlockSpec(weighted.shape, lambda j: (0, 0, 0))] + [spec for _, spec in blocks],
        out_specs=[pl.BlockSpec((rows, cols), lambda j: (0, j))] * RING,
        cost_estimate=pl.CostEstimate(
            flops=8 * stations * stations * width * days * RING, transcendentals=0, bytes_accessed=4 << 20
        ),
    )(weighted, *[a for a, _ in blocks])


def sums(weighted, q, days, stations, sources):
    like = sources[0][0][0]
    rows, width = days * stations, like.shape[1]
    steps = 2
    cols = width // steps

    def kernel(m_ref, *refs):
        tiles, outs = refs[:4], refs[4:]
        for day in range(days):
            at = pl.ds(day * stations, stations)
            mine, theirs = (stacked(tiles, n, day, stations) for n in (0, 2))
            total = dot_nn(m_ref[0], mine) + dot_nn(m_ref[1], theirs)
            outs[0][at, :] = total[:stations]
            outs[1][at, :] = total[stations:]

    blocks = [slot_blocks(source, k, rows, cols) for source in sources for k in (q, q + 2)]
    return call(
        kernel,
        grid=(steps,),
        out_shape=[jax.ShapeDtypeStruct((rows, width), jnp.float32)] * 2,
        in_specs=[pl.BlockSpec(weighted.shape, lambda j: (0, 0, 0))] + [spec for _, spec in blocks],
        out_specs=[pl.BlockSpec((rows, cols), lambda j: (0, j))] * 2,
        cost_estimate=pl.CostEstimate(
            flops=16 * stations * stations * width * days * 2, transcendentals=0, bytes_accessed=4 << 20
        ),
    )(weighted, *[a for a, _ in blocks])


def add(day_scale, total, term, k, days, stations):
    rows, width = total.shape
    steps = 2

    def kernel(w_ref, t_ref, n_ref, out):
        for day in range(days):
            at = pl.ds(day * stations, stations)
            value = w_ref[k % 2, day] * (t_ref[at, :] + n_ref[at, :].astype(jnp.float32))
            out[at, :] = value.astype(out.dtype)

    block = pl.BlockSpec((rows, width // steps), lambda j: (0, j))
    return call(
        kernel,
        grid=(steps,),
        out_shape=jax.ShapeDtypeStruct(term.shape, term.dtype),
        in_specs=[SMEM, block, block],
        out_specs=block,
        cost_estimate=pl.CostEstimate(flops=3 * rows * width, transcendentals=0, bytes_accessed=2 << 20),
    )(day_scale, total, term)


def ring_swap(x, k):
    return lax.ppermute(x, RING_AXES, [(i, i ^ k) for i in range(RING)])


def move_up(x, columns):
    return lax.ppermute(x, "h", [(i, (i + 1) % columns) for i in range(columns)])


def move_down(x, columns):
    return lax.ppermute(x, "h", [((i + 1) % columns, i) for i in range(columns)])


def move_apart(x, columns, step):
    pairs = [
        (2 * i + side, 2 * ((i + (step if side else -step)) % columns) + side) for i in range(columns) for side in (0, 1)
    ]
    return lax.ppermute(x, ("h", "xh"), pairs)


def core_swap(x):
    return lax.ppermute(x, "c", [(0, 1), (1, 0)])


def shards(spectra, pair_mask, window_of_day, band_weight):
    days, _, stations, width = spectra.shape
    columns = lax.axis_size("h")
    norm_scale = (2.0 * (width // (2 * NBAND))) ** (-0.5)
    count_first = jnp.sum((window_of_day == 0).astype(jnp.float32))
    count_second = jnp.sum((window_of_day == 1).astype(jnp.float32))
    all_weights = jnp.where(window_of_day == 0, 1.0 / count_first, -1.0 / count_second)
    by_device = all_weights.reshape(2, 2, days)
    on_core = lax.dynamic_index_in_dim(by_device, lax.axis_index("c"), 1, keepdims=False)
    day_weight = jnp.where(lax.axis_index("xl") == 0, on_core, on_core[::-1])
    day_scale = day_weight * norm_scale

    *owns, one, three, two = pack(
        spectra, pair_mask, [(((0, 0),), True), (((1, 0),), False)] + [(((0, k),), k == 2) for k in SENT]
    )
    second = pack(spectra, pair_mask, [(((1, k),), False) for k in SENT])
    came = [ring_swap(piece, k) for k, piece in zip(SENT, (one, three, two))]
    here = {"own": owns[0], "pair": join(came[:2]), "last": came[2]}
    above = {what: move_down(a, columns) for what, a in here.items()}
    below = {what: move_up(a, columns) for what, a in here.items()}
    sources = [((w["own"], 0), (w["pair"], 0), (w["last"], 0), (w["pair"], 1)) for w in (here, above, below)]
    masks = [here["own"], here["last"], below["own"], below["last"]]
    mine = powers(day_weight, 1, days, stations, sources)
    mine = powers(day_weight, 0, days, stations, sources, mine)
    weighted = weigh(0, band_weight, norm_scale, mine, core_swap(mine), masks, stations)
    moved = {}
    for q in (0, 1):
        grads = gradients(day_scale, weighted, q, days, stations, sources)
        for k, piece in zip((q, q + 2), grads):
            moved[k] = piece if k == 0 else ring_swap(piece, k)
    out = unpack(moved, 0, spectra.shape)

    slots = {0: owns[1]} | {k: ring_swap(piece, k) for k, piece in zip(SENT, second)}
    near = {k: move_apart(a, columns, 1 if k < 2 else -1) for k, a in slots.items()}
    sources = [[(w[k], 0) for k in range(RING)] for w in (slots, near)]
    masks = [w[what] for w in (here, above, below) for what in ("own", "last")]
    mine = near_powers(day_weight, 0, days, stations, sources)
    mine = near_powers(day_weight, 1, days, stations, sources, mine)
    weighted = near_weigh(1, band_weight, norm_scale, mine, core_swap(mine), masks, stations)
    sent = terms(weighted, days, stations, sources[0])
    term = [move_apart(a, columns, -1 if k < 2 else 1) for k, a in enumerate(sent)]
    total = [None] * RING
    for q in (0, 1):
        total[q], total[q + 2] = sums(weighted, q, days, stations, sources)
    moved = {}
    for k in range(RING):
        piece = add(day_scale, total[k], term[k], k, days, stations)
        moved[k] = piece if k == 0 else ring_swap(piece, k)
    out = unpack({k: moved[k] for k in (0, 1, 2)}, 1, spectra.shape, out)
    out = unpack({3: moved[3]}, 1, spectra.shape, out)
    return out


def solution(mesh):
    columns = mesh.shape["pair"] // 2
    fine = Mesh(mesh.devices.reshape(columns, 2, 2, 2), ("h", "xh", "xl", "c"))
    return jax.shard_map(
        shards,
        mesh=fine,
        in_specs=(P(("xl", "c"), ("h", "xh"), None, None), P(("h", "xh"), None), P(), P()),
        out_specs=P(("xl", "c"), ("h", "xh"), None, None),
        check_vma=False,
    )
```
